32 devices in a mesh: lon: 2 (over core), lat: 4 (over y, x), mem: 4 (over z).
Axes of the slice: x: 2, y: 2, z: 4, core: 2. Of those that a mesh axis runs over, the one named last changes fastest.
Arguments:
- ensemble: bfloat16 [80, 4, 4, 128, 512], P('mem', None, None, 'lon', 'lat'), may hold values from -6 to 6
- huber: float32 [4, 4, 128, 512], P(None, None, 'lon', 'lat'), may hold values from 0.1 to 1
- innovation: float32 [4, 4, 128, 512], P(None, None, 'lon', 'lat'), may hold values from -6 to 6
- sea_mask: int32 [32, 128], P('lon', 'lat'), may hold values 0 or 1
Outputs:
- control: float32 [80, 4, 32, 128], P('mem', None, 'lon', 'lat')
- gradient: float32 [80, 4, 32, 128], P('mem', None, 'lon', 'lat')
The draws below stay inside these ranges and needn't reach their ends.
All inputs are finite; a program needn't handle non-finite values. No bound on the sum of `sea_mask` on one device may be relied on, other than what follows from the above.
Results may differ from the reference program's by a relative error of at most 0.013.
Values may be sent and summed in bfloat16 or wider, within the bound.
No kernel may reach another device: no remote copies, remote signals or barrier semaphores. Data moves between devices by JAX's collectives and lax.ppermute only.
A program may use at most 128 MiB of HBM per device.

```python
import math
import jax
import jax.numpy as jnp
from jax import lax

MEMBERS = 80
VARS = 4
RATIO = 4
DSTEPS = 4
ITERS = 3
LEV = 4
NX = 128
NY = 512
NCX = 32
NCY = 128


def place_ends(result, key, low, top_value):
    longest = result.shape.index(max(result.shape))
    spots = []
    for shift in (0, 1):
        where = [jax.random.randint(jax.random.fold_in(key, axis), (), 0, length) for axis, length in enumerate(result.shape)]
        where[longest] = (where[longest] + shift) % result.shape[longest]
        spots.append(tuple(where))
    return result.at[spots[0]].set(low).at[spots[1]].set(top_value)


def levels(key, dims, pieces, smallest, high):
    gain = 1.0
    for axis_at, shards_of in pieces:
        heights = jax.random.uniform(jax.random.fold_in(jax.random.fold_in(key, 6), axis_at), (shards_of,), jnp.float32, smallest / len(pieces), high / len(pieces))
        gain = gain * jnp.repeat(jnp.exp(heights), dims[axis_at] // shards_of).reshape((-1,) + (1,) * (len(dims) - 1 - axis_at))
    return gain


def bell_draw(own_key, dims, width, limit, shards=(), kind=jnp.bfloat16):
    array = width * jax.random.normal(own_key, dims, jnp.float32)
    if shards:
        array = array * levels(own_key, dims, shards, -0.22, 0.18)
    return jnp.clip(array, -limit, limit).astype(kind)


def setup_inputs(seed: int = 0) -> dict:
    streams_of = jax.random.split(jax.random.key(seed), 5)
    return {
        "ensemble": bell_draw(streams_of[0], (MEMBERS, VARS, LEV, NX, NY), 1.0, 6.0, ((0, 4), (3, 2), (4, 4))),
        "huber": jnp.clip(jnp.exp(math.log(1.0) - 2.3025851 * jax.random.uniform(streams_of[1], (VARS, LEV, NX, NY), jnp.float32) ** levels(streams_of[1], (VARS, LEV, NX, NY), ((2, 2), (3, 4)), -0.2, 0.2)), 0.1, 1.0),
        "innovation": bell_draw(streams_of[2], (VARS, LEV, NX, NY), 1.0, 6.0, ((2, 2), (3, 4)), jnp.float32),
        "sea_mask": place_ends((jax.random.randint(streams_of[3], (NCX, NCY), 0, 4) < 3).astype(jnp.int32), jax.random.fold_in(streams_of[3], 1), 0, 1),
    }


diffusion_rate = 0.2

def hat_table(rows, cols, row_shift, col_shift):
    fine_pos = (jnp.arange(rows, dtype=jnp.float32) - row_shift + 0.5) / RATIO - 0.5
    coarse_pos = jnp.arange(cols, dtype=jnp.float32) - col_shift
    return jnp.maximum(0.0, 1.0 - jnp.abs(coarse_pos[None, :] - fine_pos[:, None]))

def smooth_once(padded):
    inner = padded[:, :, 1:-1, 1:-1]
    beside = padded[:, :, 2:, 1:-1] + padded[:, :, :-2, 1:-1] + padded[:, :, 1:-1, 2:] + padded[:, :, 1:-1, :-2]
    return inner + diffusion_rate * (beside - 4.0 * inner)

def diffuse(field):
    for step in range(DSTEPS):
        field = smooth_once(jnp.pad(field, ((0, 0), (0, 0), (1, 1), (1, 1))))
    return field

def forward_increment(ensemble, coarse, fine_x, fine_y):
    scale = 1.0 / math.sqrt(MEMBERS - 1)

    def add_member(total, pair):
        member, weights = pair
        fine = jnp.einsum('xc,lcd,yd->lxy', fine_x, weights, fine_y, precision=lax.Precision.HIGHEST).astype(jnp.bfloat16)
        return (total + member.astype(jnp.float32) * fine.astype(jnp.float32)[None], None)
    total, _ = lax.scan(add_member, jnp.zeros(ensemble.shape[1:], jnp.float32), (ensemble, coarse))
    return total * scale

def adjoint_coarse(ensemble, misfit, fine_x, fine_y):
    scale = 1.0 / math.sqrt(MEMBERS - 1)

    def one_member(member):
        spread = lax.optimization_barrier(jnp.sum(member.astype(jnp.float32) * misfit.astype(jnp.float32), axis=0)) * scale
        return jnp.einsum('xc,lxy,yd->lcd', fine_x, spread, fine_y, precision=lax.Precision.HIGHEST)
    return lax.map(one_member, ensemble)

def reference(ensemble, huber, innovation, sea_mask):
    keep = sea_mask.astype(jnp.float32)
    fine_x = hat_table(NX, NCX, 0, 0)
    fine_y = hat_table(NY, NCY, 0, 0)

    def hessian(field):
        shaped = diffuse(keep * field)
        total = forward_increment(ensemble, shaped, fine_x, fine_y)
        misfit = (huber * total).astype(jnp.bfloat16)
        back = adjoint_coarse(ensemble, misfit, fine_x, fine_y)
        return field + keep * diffuse(back)
    misfit_start = (huber * innovation).astype(jnp.bfloat16)
    gradient = -(keep * diffuse(adjoint_coarse(ensemble, misfit_start, fine_x, fine_y)))
    control = jnp.zeros_like(gradient)
    for step in range(ITERS):
        image = hessian(gradient)
        alpha = jnp.sum(gradient * gradient) / jnp.sum(gradient * image)
        control = control - alpha * gradient
        gradient = gradient - alpha * image
    return (control, gradient)
```

```python
import math

import jax
import jax.numpy as jnp
import numpy as np
from jax import lax
from jax.experimental import pallas as pl
from jax.experimental.pallas import tpu as pltpu
from jax.sharding import PartitionSpec as P

MEMBERS = 80
DSTEPS = 4
ITERS = 3
RATE = 0.2
LANES = 128
HALO = DSTEPS + 1
STRIP = 2 * HALO
PACK = STRIP + HALO
TERMS = DSTEPS + 1
F32 = jnp.float32
BF16 = jnp.bfloat16


def hat_table(rows, cols, col_shift, ratio):
    fine = (np.arange(rows) + 0.5) / ratio - 0.5
    coarse = np.arange(cols) - col_shift
    return np.maximum(0.0, 1.0 - np.abs(coarse[None, :] - fine[:, None]))


def axis_terms(cells, fine, devices, powers):
    ext = cells + 2 * HALO
    hat = hat_table(fine, ext, HALO, fine // cells)
    out = []
    for at in range(devices):
        where = at * cells - HALO + np.arange(ext)
        inside = ((where >= 0) & (where < cells * devices)).astype(np.float64)
        step = (0.5 - 2 * RATE) * np.eye(ext) + RATE * (np.eye(ext, k=1) + np.eye(ext, k=-1))
        step = inside[:, None] * step * inside[None, :]
        out.append([hat @ (np.diag(inside) @ np.linalg.matrix_power(step, p)) for p in powers])
    return np.array(out)


def thirds(value):
    hi = value.astype(BF16).astype(F32)
    mid = (value - hi).astype(BF16).astype(F32)
    return hi, mid, value - hi - mid


def iota(shape, axis):
    return lax.broadcasted_iota(jnp.int32, shape, axis)


def rows_of(shape, first, values):
    at = iota(shape, 0)
    out = jnp.zeros(shape, F32)
    for k, v in enumerate(values):
        out = jnp.where(at == first + k, v, out)
    return out


def build(mesh_shape, ens_shape, mask_shape):
    members, nvar, levels, fx, fy = ens_shape
    cx, cy = mask_shape
    n_lon, n_lat, n_mem = (mesh_shape[a] for a in ("lon", "lat", "mem"))
    scale = 1.0 / math.sqrt(MEMBERS - 1)
    ex, ey = cx + 2 * HALO, cy + 2 * HALO
    exp = cx + 16
    assert levels == n_mem and fy == LANES and exp >= ex + 6 and exp % 16 == 0 and members % 2 == 0
    assert cx >= STRIP and cy >= STRIP and ey <= 48 and fx % 16 == 0
    fields = levels * members

    def packing(width):
        groups = next(g for g in range(1, fields + 1) if fields % g == 0 and (fields // g) * width <= LANES)
        return groups, fields // groups

    krows = TERMS * exp
    klanes = TERMS * LANES

    coef = [math.comb(DSTEPS, k) for k in range(TERMS)]
    ax = axis_terms(cx, fx, n_lon, range(TERMS))
    by = axis_terms(cy, fy, n_lat, [DSTEPS - k for k in range(TERMS)])
    a_np = np.zeros((n_lon, fx, TERMS, exp))
    a_np[..., :ex] = np.moveaxis(ax, 1, 2) * np.array(coef)[None, None, :, None]
    a_np = a_np.reshape(n_lon, fx, krows)
    b_np = np.zeros((n_lat, TERMS, fy, LANES))
    b_np[..., :ey] = by
    b_np = b_np.reshape(n_lat, klanes, LANES)
    def halves(table):
        hi = table.astype(BF16).astype(np.float64)
        return hi, table - hi

    a_tab = jnp.asarray(a_np, BF16)
    at_tab = jnp.asarray(np.concatenate(halves(np.swapaxes(a_np, 1, 2)), axis=2), BF16)
    b_hi, b_lo = halves(b_np)
    b_both = b_hi + np.roll(b_lo, 64, axis=2)
    bn_tab = jnp.asarray(b_both, BF16)
    bt_tab = jnp.asarray(np.swapaxes(b_both, 1, 2), BF16)

    prows = nvar * fx
    chunks = fx // 16
    sds = jax.ShapeDtypeStruct
    vmem = pl.BlockSpec(memory_space=pltpu.VMEM)
    smem = pl.BlockSpec(memory_space=pltpu.SMEM)

    def level(j, ix):
        return lax.rem(ix[0] + j, levels)

    def call(body, name, ins, shapes, scratch=()):
        return pl.pallas_call(
            body,
            name=name,
            in_specs=[smem] + [vmem] * ins,
            out_specs=[vmem] * len(shapes),
            out_shape=shapes,
            scratch_shapes=scratch,
            compiler_params=pltpu.CompilerParams(vmem_limit_bytes=16 << 20),
        )

    payload = sds((prows + 16, fy), BF16)
    small = sds((8, LANES), F32)

    def forward(d):
        def body(ix, ens, g, keep, a, bt, gg, out, t, w):
            lev = level(d, ix)
            field = g[d * members : (d + 1) * members] * keep[...][None]
            field = (field + pltpu.roll(field, 64, 2)).reshape(members * exp, LANES).astype(BF16)
            t[...] = jnp.dot(field, bt[ix[2]], preferred_element_type=F32).astype(BF16)
            for m in range(0, members, 2):
                rhs = jnp.concatenate(
                    [
                        jnp.concatenate(
                            [t[(m + i) * exp : (m + i + 1) * exp, k * LANES : (k + 1) * LANES] for i in range(2)],
                            axis=1,
                        )
                        for k in range(TERMS)
                    ],
                    axis=0,
                )
                pair = jnp.dot(a[ix[1]], rhs, preferred_element_type=F32)
                w[m] = pair[:, :LANES].astype(BF16)
                w[m + 1] = pair[:, LANES:].astype(BF16)

            def chunk(c, carry):
                at = pl.multiple_of(c * 16, 16)
                acc = jnp.zeros((nvar, 16, fy), F32)
                for m in range(members):
                    acc = acc + ens[m, :, lev, pl.ds(at, 16), :].astype(F32) * w[m, pl.ds(at, 16), :].astype(F32)[None]
                for v in range(nvar):
                    out[pl.ds(pl.multiple_of(v * fx + at, 16), 16), :] = acc[v].astype(BF16)
                return carry

            lax.fori_loop(0, chunks, chunk, 0)
            out[pl.ds(prows, 16), :] = rows_of((16, LANES), 0, thirds(gg[0:1, :])).astype(BF16)

        scratch = [pltpu.VMEM((members * exp, klanes), BF16), pltpu.VMEM((members, fx, fy), BF16)]
        return call(body, f"forward{d}", 6, [payload], scratch)

    def misfit_body(ix, huber, *rest):
        parts, (out, gg) = rest[:levels], rest[levels:]
        total = parts[0][...].astype(F32)
        for p in parts[1:]:
            total = total + p[...].astype(F32)
        weight = huber[:, ix[0]].reshape(prows, fy)
        out[...] = (weight * (total[:prows] * scale)).astype(BF16)
        tail = total[prows:]
        gg[...] = jnp.broadcast_to(tail[0:1] + tail[1:2] + tail[2:3], (8, LANES))

    misfit_own = call(misfit_body, "misfit", 1 + levels, [sds((prows, fy), BF16), small])

    def adjoint_core(ens, lev, mis, at, bn, sp, zs):
        def chunk(c, carry):
            row = pl.multiple_of(c * 16, 16)
            mv = [mis[pl.ds(pl.multiple_of(v * fx + row, 16), 16), :].astype(F32) for v in range(nvar)]
            for m in range(members):
                s = ens[m, 0, lev, pl.ds(row, 16), :].astype(F32) * mv[0]
                for v in range(1, nvar):
                    s = s + ens[m, v, lev, pl.ds(row, 16), :].astype(F32) * mv[v]
                s = s.astype(BF16)
                sp[pl.ds(row, 16), pl.ds(m * LANES, LANES)] = s
                sp[pl.ds(pl.multiple_of(fx + row, 16), 16), pl.ds(m * LANES, LANES)] = s
            return carry

        lax.fori_loop(0, chunks, chunk, 0)
        for m in range(0, members, 2):
            z = jnp.dot(at, sp[:, m * LANES : (m + 2) * LANES], preferred_element_type=F32).astype(BF16)
            for i in range(2):
                for k in range(TERMS):
                    zs[(m + i) * exp : (m + i + 1) * exp, k * LANES : (k + 1) * LANES] = z[
                        k * exp : (k + 1) * exp, i * LANES : (i + 1) * LANES
                    ]
        both = jnp.dot(zs[...], bn, preferred_element_type=F32) * scale
        lane = iota((1, LANES), 1)
        res = jnp.where(lane < 64, both + pltpu.roll(both, 64, 1), 0.0)
        return res.reshape(members, exp, LANES)

    n_strips = 1 if n_lon == 2 else 2

    def strips_of(lon, block, tail):
        lo, hi = block[:, :16], block[:, cx : cx + 16]
        sends = [jnp.where(lon == 0, hi, lo)] if n_lon == 2 else [hi, lo]
        row = iota((1, 16, 1), 1) < STRIP
        return [jnp.where(row, s, tail[None]) for s in sends]

    part_shape = sds((members, exp, LANES), F32)

    strip_shape = sds((fields, 16, LANES), F32)

    adj_scratch = [
        pltpu.VMEM((2 * fx, members * LANES), BF16),
        pltpu.VMEM((members * exp, klanes), BF16),
    ]

    def first_body(ix, ens, huber, innov, at, bn, extra, q, *rest):
        strips, (mis, sp, zs) = rest[:n_strips], rest[n_strips:]
        j = pl.program_id(0)
        mis[...] = (huber[:, 0] * innov[:, 0]).astype(BF16).reshape(prows, fy)
        res = adjoint_core(ens, 0, mis, at[0], bn[0], sp, zs)
        here = (iota((members, 1, 1), 0) == 0) & (j == 0)
        res = res + jnp.where(here, extra[...][None], 0.0)
        q[0] = res
        for ref, val in zip(strips, strips_of(ix[1], res, jnp.zeros((16, LANES), F32))):
            ref[...] = val

    def table(arr, slot):
        return pl.BlockSpec((1,) + arr.shape[1:], lambda j, ix: (ix[slot], 0, 0))

    obs_spec = pl.BlockSpec((nvar, 1, fx, fy), lambda j, ix: (0, level(j, ix), 0, 0))
    first_adjoint = pl.pallas_call(
        first_body,
        name="first_adjoint",
        out_shape=[sds((levels, members, exp, LANES), F32)] + [strip_shape] * n_strips,
        grid_spec=pltpu.PrefetchScalarGridSpec(
            num_scalar_prefetch=1,
            grid=(levels,),
            in_specs=[
                pl.BlockSpec((members, nvar, 1, fx, fy), lambda j, ix: (0, 0, level(j, ix), 0, 0)),
                obs_spec,
                obs_spec,
                table(at_tab, 1),
                table(bn_tab, 2),
                pl.BlockSpec((exp, LANES), lambda j, ix: (0, 0)),
            ],
            out_specs=[pl.BlockSpec((1, members, exp, LANES), lambda j, ix: (j, 0, 0, 0))]
            + [pl.BlockSpec((members, 16, LANES), lambda j, ix: (j, 0, 0))] * n_strips,
            scratch_shapes=[pltpu.VMEM((prows, fy), BF16)] + adj_scratch,
        ),
        compiler_params=pltpu.CompilerParams(vmem_limit_bytes=24 << 20),
    )

    def adjoint(d, others):
        def body(ix, ens, huber, at, bn, mis, *rest):
            final = others > 0
            if final:
                gg, rest = rest[0], rest[1:]
                qs, parts, rest = rest[:others], rest[others : 2 * others], rest[2 * others :]
            q, sums, rest = rest[0], rest[1], rest[2:]
            strips, (sp, zs) = rest[: n_strips * final], rest[n_strips * final :]
            lev = level(d, ix)
            value = mis[...].astype(F32)
            part = jnp.sum(value * value / huber[:, lev].reshape(prows, fy), axis=0, keepdims=True)
            part = jnp.broadcast_to(jnp.sum(part, axis=1, keepdims=True), (1, LANES))
            res = adjoint_core(ens, lev, mis, at[ix[1]], bn[ix[2]], sp, zs)
            q[...] = res
            if not final:
                sums[...] = jnp.broadcast_to(part, (8, LANES))
                return
            for p in parts:
                part = part + p[0:1]
            sums[...] = rows_of((8, LANES), 0, [gg[0:1, :], part])
            tail = rows_of((16, LANES), STRIP, [*thirds(gg[0:1, :]), *thirds(part)])
            for lvl, ref in [(order[i], qs[i]) for i in range(others)] + [(d, q)]:
                for out, val in zip(strips, strips_of(ix[1], ref[...], tail)):
                    out[lvl * members : (lvl + 1) * members] = val

        final = others > 0
        shapes = [part_shape, small] + [strip_shape] * (n_strips * final)
        return call(body, f"adjoint{d}", 5 + (1 + 2 * others) * final, shapes, adj_scratch)

    order = [0] + [d for d in (1, levels - 1) if d > 0 and d < levels]
    order = list(dict.fromkeys(order))
    order = order + [d for d in range(levels) if d not in order]

    full_q = (fields, exp, LANES)

    def masks(ix, slot, size):
        at = ix[slot]
        return (at > 0).astype(F32), (at < size - 1).astype(F32)

    def tail_sums(tail, row):
        t = [tail[row + k : row + k + 1].astype(F32) for k in range(6)]
        return t[0] + t[1] + t[2], t[3] + t[4] + t[5]

    def lon_join(first, last):
        kind = F32 if last else BF16
        width = HALO if last else PACK
        groups, packs = packing(width)
        src_hi = cy + HALO if last else cy

        def body(ix, *rest):
            if first:
                q_in, rest = [rest[0].at[d] for d in range(levels)], rest[1:]
            else:
                q_in, sc, rest = rest[:levels], rest[levels], rest[levels + 1 :]
            recv, (out, to_next, to_prev, *sums) = rest[:n_strips], rest[n_strips:]
            has_lo, has_hi = masks(ix, 1, n_lon)
            if not first:
                total = sc[...]
                for r in recv:
                    total = total + rows_of((8, LANES), 0, tail_sums(r[fields - 1], STRIP))
                sums[0][...] = total
            strip_rows = iota((1, 16, 1), 1) < STRIP

            def joined(mine, theirs, here):
                return jnp.where(strip_rows & (here > 0), mine + theirs, mine)

            for d in range(levels):
                at = slice(d * members, (d + 1) * members)
                q = q_in[d]
                out[at, 0:16, :] = joined(q[:, 0:16, :], recv[0][at], has_lo)
                for r0 in range(16, cx, 16):
                    out[at, r0 : r0 + 16, :] = q[:, r0 : r0 + 16, :]
                out[at, cx : cx + 16, :] = joined(q[:, cx : cx + 16, :], recv[-1][at], has_hi)
            lane = iota((1, 1, LANES), 2)
            nxt = jnp.zeros((groups, exp, LANES), F32)
            prv = jnp.zeros((groups, exp, LANES), F32)
            for p in range(packs):
                block = out[p * groups : (p + 1) * groups]
                at = p * width
                wide = HALO if last else STRIP
                here = (lane >= at) & (lane < at + wide)
                prv = jnp.where(here, pltpu.roll(block, at % LANES, 2), prv)
                nxt = jnp.where(here, pltpu.roll(block, (at - src_hi) % LANES, 2), nxt)
                if not last:
                    low = block - block.astype(BF16).astype(F32)
                    here = (lane >= at + STRIP) & (lane < at + PACK)
                    prv = jnp.where(here, pltpu.roll(low, (at + STRIP - HALO) % LANES, 2), prv)
                    nxt = jnp.where(here, pltpu.roll(low, (at + STRIP - cy) % LANES, 2), nxt)
            if first:
                to_next[0:groups] = nxt.astype(kind)
                to_prev[0:groups] = prv.astype(kind)
                to_prev[groups] = pltpu.roll(out[0], LANES - 64, 1).astype(kind)
                to_next[groups] = pltpu.roll(out[0], LANES - 64 - cy, 1).astype(kind)
            else:
                tail = rows_of((exp, LANES), ex, [*thirds(total[0:1]), *thirds(total[1:2])])[None]
                row = iota((1, exp, 1), 1) >= ex
                to_next[0:groups] = jnp.where(row, tail, nxt).astype(kind)
                to_prev[0:groups] = jnp.where(row, tail, prv).astype(kind)

        shapes = [sds(full_q, F32)] + [sds((groups + first, exp, LANES), kind)] * 2 + ([] if first else [small])
        ins = (1 if first else levels + 1) + n_strips
        return call(body, "lon_first" if first else "lon_last" if last else "lon", ins, shapes)

    far = list(range(2, n_lat - 1))

    def gathered(ix, q, from_prev, from_next, p, last):
        width = HALO if last else PACK
        groups, _ = packing(width)
        has_lo, has_hi = masks(ix, 2, n_lat)
        lane = iota((1, 1, LANES), 2)
        mine = q[p * groups : (p + 1) * groups]
        from_prev, from_next = from_prev[0:groups], from_next[0:groups]

        def put(total, packed, start, here, wide, where):
            ok = (lane >= start) & (lane < start + wide) & (here > 0)
            return total + jnp.where(ok, pltpu.roll(packed, (start - where) % LANES, 2), 0.0)

        at = p * width
        if last:
            mine = put(mine, from_prev, HALO, has_lo, HALO, at)
            return put(mine, from_next, cy, has_hi, HALO, at)
        mine = put(mine, from_prev, 0, has_lo, STRIP, at)
        mine = put(mine, from_prev, 0, has_lo, HALO, at + STRIP)
        mine = put(mine, from_next, cy, has_hi, STRIP, at)
        return put(mine, from_next, cy + HALO, has_hi, HALO, at + STRIP)

    def own_cells():
        row, lane = iota((exp, LANES), 0), iota((exp, LANES), 1)
        inside = (row >= HALO) & (row < HALO + cx) & (lane >= HALO) & (lane < HALO + cy)
        return inside.astype(F32)

    def start_body(ix, q, r_prev, r_next, g_out, keep_out, gg):
        groups, packs = packing(PACK)
        from_prev, from_next = r_prev[...].astype(F32), r_next[...].astype(F32)
        has_lo, has_hi = masks(ix, 2, n_lat)
        lane = iota((exp, LANES), 1)
        row = iota((exp, LANES), 0)
        mine = pltpu.roll(q[0], LANES - 64, 1)
        lo = from_prev[groups]
        hi = pltpu.roll(from_next[groups], cy, 1)
        keep = jnp.where(lane < ey, mine, 0.0)
        keep = keep + jnp.where((lane < STRIP) & (has_lo > 0), lo, 0.0)
        keep = keep + jnp.where((lane >= cy) & (lane < ey) & (has_hi > 0), hi, 0.0)
        keep = jnp.where(row < ex, keep, 0.0)
        keep_out[...] = keep
        acc = jnp.zeros((exp, LANES), F32)
        for p in range(packs):
            g = -(keep[None] * gathered(ix, q, from_prev, from_next, p, False))
            g_out[p * groups : (p + 1) * groups] = g
            acc = acc + jnp.sum(g * g, axis=0)
        gg[...] = jnp.broadcast_to(jnp.sum(acc * own_cells()), (8, LANES))

    g_shape = sds(full_q, F32)
    start_step = call(start_body, "start_step", 3, [g_shape, sds((exp, LANES), F32), small])
    final_shape = sds((members, levels, cx, cy), F32)

    def step(first, last):
        groups, packs = packing(HALO if last else PACK)

        def body(ix, q, r_prev, r_next, sums, keep, g, *rest):
            tiny, rest = rest[: len(far)], rest[len(far) :]
            if not first:
                c_in, rest = rest[0], rest[1:]
            g_out, c_out = rest[:2]
            from_prev, from_next = r_prev[...].astype(F32), r_next[...].astype(F32)
            total = sums[...]
            for ref in tiny:
                total = total + ref[...]
            gg, dot = total[0:1], total[1:2]
            for ref in [r_prev, r_next] if n_lat > 2 else [r_next] if n_lat == 2 else []:
                more = tail_sums(ref[0], ex)
                gg, dot = gg + more[0], dot + more[1]
            alpha = (gg / (gg + dot))[None]
            kept = keep[...][None]
            acc = jnp.zeros((exp, LANES), F32)
            for p in range(packs):
                at = slice(p * groups, (p + 1) * groups)
                old = g[at]
                image = old + kept * gathered(ix, q, from_prev, from_next, p, last)
                new = old - alpha * image
                ctl = -alpha * old if first else c_in[at] - alpha * old
                if not last:
                    g_out[at] = new
                    c_out[at] = ctl
                    acc = acc + jnp.sum(new * new, axis=0)
                else:
                    for ref, val in ((g_out, new), (c_out, ctl)):
                        val = pltpu.roll(pltpu.roll(val, LANES - HALO, 2), exp - HALO, 1)
                        for i in range(groups):
                            f = p * groups + i
                            ref[f % members, level(f // members, ix)] = val[i, :cx, :cy]
            if not last:
                rest[2][...] = jnp.broadcast_to(jnp.sum(acc * own_cells()), (8, LANES))

        shapes = [final_shape] * 2 if last else [g_shape, g_shape, small]
        return call(body, "last_step" if last else "step", 6 + len(far) + (not first), shapes)

    def ring(size, d):
        return [(i, (i + d) % size) for i in range(size)]

    def exchange(qs, strips, sc, ix, first, last):
        if n_lon == 2:
            recv = [lax.ppermute(strips[0], "lon", ring(2, 1))]
        else:
            recv = [lax.ppermute(strips[0], "lon", ring(n_lon, 1)), lax.ppermute(strips[1], "lon", ring(n_lon, -1))]
        out, to_next, to_prev, *sums = lon_join(first, last)(ix, *qs, *sc, *recv)
        if not first and n_lon > 2:
            for d in range(2, n_lon - 1):
                sums[0] = sums[0] + lax.ppermute(sc[0], "lon", ring(n_lon, d))
        from_prev = lax.ppermute(to_next, "lat", ring(n_lat, 1))
        from_next = lax.ppermute(to_prev, "lat", ring(n_lat, -1))
        tiny = [] if first else [lax.ppermute(sums[0], "lat", ring(n_lat, d)) for d in far]
        return out, from_prev, from_next, sums, tiny

    def local(ensemble, huber, innovation, sea_mask):
        slot = lax.broadcasted_iota(jnp.int32, (3,), 0)
        ix = jnp.where(
            slot == 0,
            lax.axis_index("mem"),
            jnp.where(slot == 1, lax.axis_index("lon"), lax.axis_index("lat")),
        ).astype(jnp.int32)
        extra = jnp.pad(
            sea_mask.astype(F32),
            ((HALO, exp - HALO - cx), (64 + HALO, LANES - 64 - HALO - cy)),
        )
        far_off = [pltpu.with_memory_space_constraint(x, pltpu.HBM) for x in (ensemble, huber, innovation, at_tab, bn_tab)]
        q, *strips = first_adjoint(ix, *far_off, extra)
        q, r_prev, r_next, _, _ = exchange([q], strips, [], ix, True, False)
        g, keep, gg = start_step(ix, q, r_prev, r_next)
        control = []
        sends = sorted(range(1, n_mem), key=lambda d: (-min(d, n_mem - d), d))
        for it in range(ITERS):
            last = it == ITERS - 1
            parts = {d: forward(d)(ix, ensemble, g, keep, a_tab, bt_tab, gg)[0] for d in sends + [0]}
            moved = {d: lax.ppermute(parts[d], "mem", ring(n_mem, d)) for d in sends}
            mis, ggm = misfit_own(ix, huber, parts[0], *[moved[d] for d in sends])
            every = {d: lax.ppermute(mis, "mem", ring(n_mem, -d)) for d in sends}
            every[0] = mis
            qs, dots = [], []
            for d in order[:-1]:
                q, dot = adjoint(d, 0)(ix, ensemble, huber, at_tab, bn_tab, every[d])
                qs.append(q)
                dots.append(dot)
            d = order[-1]
            q, sc, *strips = adjoint(d, levels - 1)(
                ix, ensemble, huber, at_tab, bn_tab, every[d], ggm, *qs, *dots
            )
            by_level = dict(zip(order, qs + [q]))
            q, r_prev, r_next, sums, tiny = exchange(
                [by_level[d] for d in range(levels)], strips, [sc], ix, False, last
            )
            out = step(it == 0, last)(ix, q, r_prev, r_next, *sums, keep, g, *tiny, *control)
            if last:
                return out[1], out[0]
            g, control, gg = out[0], [out[1]], out[2]

    return local


def solution(mesh):
    placed = (
        P("mem", None, None, "lon", "lat"),
        P(None, None, "lon", "lat"),
        P(None, None, "lon", "lat"),
        P("lon", "lat"),
    )

    def local(ensemble, huber, innovation, sea_mask):
        return build(dict(mesh.shape), ensemble.shape, sea_mask.shape)(ensemble, huber, innovation, sea_mask)

    return jax.shard_map(
        local,
        mesh=mesh,
        in_specs=placed,
        out_specs=(P("mem", None, "lon", "lat"), P("mem", None, "lon", "lat")),
        check_vma=False,
    )
```

```python
import math

import jax
import jax.numpy as jnp
import numpy as np
from jax import lax
from jax.experimental import pallas as pl
from jax.experimental.pallas import tpu as pltpu
from jax.sharding import PartitionSpec as P


MEMBERS = 80
DSTEPS = 4
ITERS = 3
RATE = 0.2
LANES = 128
HALO = DSTEPS + 1
STRIP = 2 * HALO
PACK = STRIP + HALO
TERMS = DSTEPS + 1
F32 = jnp.float32
BF16 = jnp.bfloat16


def hat_table(rows, cols, col_shift, ratio):
    fine = (np.arange(rows) + 0.5) / ratio - 0.5
    coarse = np.arange(cols) - col_shift
    return np.maximum(0.0, 1.0 - np.abs(coarse[None, :] - fine[:, None]))


def axis_terms(cells, fine, devices, powers):
    ext = cells + 2 * HALO
    hat = hat_table(fine, ext, HALO, fine // cells)
    out = []
    for at in range(devices):
        where = at * cells - HALO + np.arange(ext)
        inside = ((where >= 0) & (where < cells * devices)).astype(np.float64)
        step = (0.5 - 2 * RATE) * np.eye(ext) + RATE * (np.eye(ext, k=1) + np.eye(ext, k=-1))
        step = inside[:, None] * step * inside[None, :]
        out.append([hat @ (np.diag(inside) @ np.linalg.matrix_power(step, p)) for p in powers])
    return np.array(out)


def thirds(value):
    hi = value.astype(BF16).astype(F32)
    mid = (value - hi).astype(BF16).astype(F32)
    return hi, mid, value - hi - mid


def iota(shape, axis):
    return lax.broadcasted_iota(jnp.int32, shape, axis)


def rows_of(shape, first, values):
    at = iota(shape, 0)
    out = jnp.zeros(shape, F32)
    for k, v in enumerate(values):
        out = jnp.where(at == first + k, v, out)
    return out


def build(mesh_shape, ens_shape, mask_shape):
    members, nvar, levels, fx, fy = ens_shape
    cx, cy = mask_shape
    n_lon, n_lat, n_mem = (mesh_shape[a] for a in ("lon", "lat", "mem"))
    scale = 1.0 / math.sqrt(MEMBERS - 1)
    ex, ey = cx + 2 * HALO, cy + 2 * HALO
    exp = cx + 16
    assert levels == n_mem and n_mem & (n_mem - 1) == 0 and n_lat % 2 == 0 and fy == LANES and exp >= ex + 6 and exp % 16 == 0 and members % 2 == 0
    assert cx >= STRIP and cy >= STRIP and ey <= 48 and fx % 16 == 0
    fields = levels * members

    def packing(width):
        groups = next(g for g in range(1, fields + 1) if fields % g == 0 and (fields // g) * width <= LANES)
        return groups, fields // groups

    krows = TERMS * exp
    klanes = TERMS * LANES

    coef = [math.comb(DSTEPS, k) for k in range(TERMS)]
    ax = axis_terms(cx, fx, n_lon, range(TERMS))
    by = axis_terms(cy, fy, n_lat, [DSTEPS - k for k in range(TERMS)])
    a_np = np.zeros((n_lon, fx, TERMS, exp))
    a_np[..., :ex] = np.moveaxis(ax, 1, 2) * np.array(coef)[None, None, :, None]
    a_np = a_np.reshape(n_lon, fx, krows)
    b_np = np.zeros((n_lat, TERMS, fy, LANES))
    b_np[..., :ey] = by
    b_np = b_np.reshape(n_lat, klanes, LANES)

    def halves(table):
        hi = table.astype(BF16).astype(np.float64)
        return hi, table - hi

    a_tab = jnp.asarray(a_np, BF16)
    at_tab = jnp.asarray(np.concatenate(halves(np.swapaxes(a_np, 1, 2)), axis=2), BF16)
    b_hi, b_lo = halves(b_np)
    b_both = b_hi + np.roll(b_lo, 64, axis=2)
    bn_tab = jnp.asarray(b_both, BF16)
    bt_tab = jnp.asarray(np.swapaxes(b_both, 1, 2), BF16)

    prows = nvar * fx
    chunks = fx // 16
    sds = jax.ShapeDtypeStruct
    vmem = pl.BlockSpec(memory_space=pltpu.VMEM)

    def level(j, ix):
        return lax.bitwise_xor(ix[0], j)

    def call(body, ins, shapes, scratch=()):
        def placed(*refs):
            return body([lax.axis_index(a) for a in ("mem", "lon", "lat")], *refs)

        return pl.pallas_call(
            placed,
            in_specs=[vmem] * ins,
            out_specs=[vmem] * len(shapes),
            out_shape=shapes,
            scratch_shapes=scratch,
            compiler_params=pltpu.CompilerParams(vmem_limit_bytes=16 << 20),
        )

    payload = sds((prows + 16, fy), BF16)
    small = sds((8, LANES), F32)

    def forward(d):
        def body(ix, ens, g, keep, a, bt, gg, out, t, w):
            lev = level(d, ix)
            field = g[d * members : (d + 1) * members] * keep[...][None]
            field = (field + pltpu.roll(field, 64, 2)).reshape(members * exp, LANES).astype(BF16)
            t[...] = jnp.dot(field, bt[ix[2]], preferred_element_type=F32).astype(BF16)
            for m in range(0, members, 2):
                rhs = jnp.concatenate(
                    [
                        jnp.concatenate(
                            [t[(m + i) * exp : (m + i + 1) * exp, k * LANES : (k + 1) * LANES] for i in range(2)],
                            axis=1,
                        )
                        for k in range(TERMS)
                    ],
                    axis=0,
                )
                pair = jnp.dot(a[ix[1]], rhs, preferred_element_type=F32)
                w[m] = pair[:, :LANES].astype(BF16)
                w[m + 1] = pair[:, LANES:].astype(BF16)

            def chunk(c, carry):
                at = pl.multiple_of(c * 16, 16)
                acc = [None] * nvar
                for m in range(members):
                    weight = w[m, pl.ds(at, 16), :].astype(F32)
                    for v in range(nvar):
                        more = ens[m, v, lev, pl.ds(at, 16), :].astype(F32) * weight
                        acc[v] = more if m == 0 else acc[v] + more
                for v in range(nvar):
                    out[pl.ds(pl.multiple_of(v * fx + at, 16), 16), :] = acc[v].astype(BF16)
                return carry

            lax.fori_loop(0, chunks, chunk, 0)
            out[pl.ds(prows, 16), :] = rows_of((16, LANES), 0, thirds(gg[0:1, :])).astype(BF16)

        scratch = [pltpu.VMEM((members * exp, klanes), BF16), pltpu.VMEM((members, fx, fy), BF16)]
        return call(body, 6, [payload], scratch)

    def misfit_body(ix, huber, *rest):
        parts, (out, gg) = rest[:levels], rest[levels:]
        total = parts[0][...].astype(F32)
        for p in parts[1:]:
            total = total + p[...].astype(F32)
        weight = huber[:, ix[0]].reshape(prows, fy)
        out[...] = (weight * (total[:prows] * scale)).astype(BF16)
        tail = total[prows:]
        gg[...] = jnp.broadcast_to(tail[0:1] + tail[1:2] + tail[2:3], (8, LANES))

    misfit_own = call(misfit_body, 1 + levels, [sds((prows, fy), BF16), small])

    def adjoint_core(ens, lev, mis, at, bn, sp, zs):
        def chunk(c, carry):
            row = pl.multiple_of(c * 16, 16)
            mv = [mis[pl.ds(pl.multiple_of(v * fx + row, 16), 16), :].astype(F32) for v in range(nvar)]
            for m in range(members):
                s = ens[m, 0, lev, pl.ds(row, 16), :].astype(F32) * mv[0]
                for v in range(1, nvar):
                    s = s + ens[m, v, lev, pl.ds(row, 16), :].astype(F32) * mv[v]
                s = s.astype(BF16)
                sp[pl.ds(row, 16), pl.ds(m * LANES, LANES)] = s
                sp[pl.ds(pl.multiple_of(fx + row, 16), 16), pl.ds(m * LANES, LANES)] = s
            return carry

        lax.fori_loop(0, chunks, chunk, 0)
        for m in range(0, members, 2):
            z = jnp.dot(at, sp[:, m * LANES : (m + 2) * LANES], preferred_element_type=F32).astype(BF16)
            for i in range(2):
                for k in range(TERMS):
                    zs[(m + i) * exp : (m + i + 1) * exp, k * LANES : (k + 1) * LANES] = z[
                        k * exp : (k + 1) * exp, i * LANES : (i + 1) * LANES
                    ]
        both = jnp.dot(zs[...], bn, preferred_element_type=F32) * scale
        lane = iota((1, LANES), 1)
        res = jnp.where(lane < 64, both + pltpu.roll(both, 64, 1), 0.0)
        return res.reshape(members, exp, LANES)

    n_strips = 1 if n_lon == 2 else 2

    def strips_of(lon, block, tail):
        lo, hi = block[:, :16], block[:, cx : cx + 16]
        sends = [jnp.where(lon == 0, hi, lo)] if n_lon == 2 else [hi, lo]
        row = iota((1, 16, 1), 1) < STRIP
        left = iota((1, 1, LANES), 2) < 64
        half = members // 2
        pairs = [jnp.where(left, s[:half], pltpu.roll(s[half:], 64, 2)) for s in sends]
        return [jnp.where(row, s, tail[None]) for s in pairs]

    part_shape = sds((members, exp, LANES), F32)

    slots = fields // 2

    def strip_shape(first):
        return sds((slots + first * levels, 16, LANES), F32)


    adj_scratch = [
        pltpu.VMEM((2 * fx, members * LANES), BF16),
        pltpu.VMEM((members * exp, klanes), BF16),
    ]

    def first_body(ix, ens, huber, innov, at, bn, extra, q, recip, *rest):
        strips, (mis, sp, zs) = rest[:n_strips], rest[n_strips:]
        recip[0] = (1.0 / huber[:, 0]).reshape(prows, fy)
        j = pl.program_id(0)
        mis[...] = (huber[:, 0] * innov[:, 0]).astype(BF16).reshape(prows, fy)
        res = adjoint_core(ens, 0, mis, at[0], bn[0], sp, zs)
        q[0] = res

        @pl.when(j == 0)
        def _():
            q[0, 0, HALO : HALO + cx, 64 + HALO : 64 + HALO + cy] = extra[...].astype(F32)

        for ref, val in zip(strips, strips_of(ix[1], res, jnp.zeros((16, LANES), F32))):
            ref[0 : members // 2] = val
        lo, hi = q[0, 0, :16], q[0, 0, cx : cx + 16]
        for ref, val in zip(strips, [jnp.where(ix[1] == 0, hi, lo)] if n_lon == 2 else [hi, lo]):
            ref[members // 2] = val

    def table(arr, slot):
        return pl.BlockSpec((1,) + arr.shape[1:], lambda j, ix: (ix[slot], 0, 0))

    obs_spec = pl.BlockSpec((nvar, 1, fx, fy), lambda j, ix: (0, level(j, ix), 0, 0))
    first_adjoint = pl.pallas_call(
        first_body,
        name="first_adjoint",
        out_shape=[sds((levels, members, exp, LANES), F32), sds((levels, prows, fy), F32)] + [strip_shape(True)] * n_strips,
        grid_spec=pltpu.PrefetchScalarGridSpec(
            num_scalar_prefetch=1,
            grid=(levels,),
            in_specs=[
                pl.BlockSpec((members, nvar, 1, fx, fy), lambda j, ix: (0, 0, level(j, ix), 0, 0)),
                obs_spec,
                obs_spec,
                table(at_tab, 1),
                table(bn_tab, 2),
                pl.BlockSpec((cx, cy), lambda j, ix: (0, 0)),
            ],
            out_specs=[
                pl.BlockSpec((1, members, exp, LANES), lambda j, ix: (j, 0, 0, 0)),
                pl.BlockSpec((1, prows, fy), lambda j, ix: (j, 0, 0)),
            ]
            + [pl.BlockSpec((members // 2 + 1, 16, LANES), lambda j, ix: (j, 0, 0))] * n_strips,
            scratch_shapes=[pltpu.VMEM((prows, fy), BF16)] + adj_scratch,
        ),
        compiler_params=pltpu.CompilerParams(vmem_limit_bytes=24 << 20),
    )

    def adjoint(d, others):
        def body(ix, ens, recip, at, bn, mis, *rest):
            final = others > 0
            if final:
                gg, rest = rest[0], rest[1:]
                qs, parts, rest = rest[:others], rest[others : 2 * others], rest[2 * others :]
            q, sums, rest = rest[0], rest[1], rest[2:]
            strips, (sp, zs) = rest[: n_strips * final], rest[n_strips * final :]
            lev = level(d, ix)
            value = mis[...].astype(F32)
            part = jnp.sum(value * value * recip[d], axis=0, keepdims=True)
            part = jnp.broadcast_to(jnp.sum(part, axis=1, keepdims=True), (1, LANES))
            res = adjoint_core(ens, lev, mis, at[ix[1]], bn[ix[2]], sp, zs)
            q[...] = res
            if not final:
                sums[...] = jnp.broadcast_to(part, (8, LANES))
                return
            for p in parts:
                part = part + p[0:1]
            sums[...] = rows_of((8, LANES), 0, [gg[0:1, :], part])
            tail = rows_of((16, LANES), STRIP, [*thirds(gg[0:1, :]), *thirds(part)])
            for lvl, ref in [(order[i], qs[i]) for i in range(others)] + [(d, q)]:
                for out, val in zip(strips, strips_of(ix[1], ref[...], tail)):
                    out[lvl * (members // 2) : (lvl + 1) * (members // 2)] = val

        final = others > 0
        shapes = [part_shape, small] + [strip_shape(False)] * (n_strips * final)
        return call(body, 5 + (1 + 2 * others) * final, shapes, adj_scratch)

    order = list(range(levels))

    full_q = (fields, exp, LANES)

    def masks(ix, slot, size):
        at = ix[slot]
        return (at > 0).astype(F32), (at < size - 1).astype(F32)

    def tail_sums(tail, row):
        t = [tail[row + k : row + k + 1].astype(F32) for k in range(6)]
        return t[0] + t[1] + t[2], t[3] + t[4] + t[5]

    def lon_join(first, last):
        kind = F32 if last else BF16
        width = HALO if last else PACK
        groups, packs = packing(width)
        src_hi = cy + HALO if last else cy

        def body(ix, *rest):
            if first:
                q_in, rest = [rest[0].at[d] for d in range(levels)], rest[1:]
            else:
                q_in, sc, rest = rest[:levels], rest[levels], rest[levels + 1 :]
            recv, (out, to_even, to_odd, *sums) = rest[:n_strips], rest[n_strips:]
            flip = lax.rem(ix[2], 2) == 1
            has_lo, has_hi = masks(ix, 1, n_lon)
            if not first:
                total = sc[...]
                for r in recv:
                    total = total + rows_of((8, LANES), 0, tail_sums(r[slots - 1], STRIP))
                sums[0][...] = total
            strip_rows = iota((1, 16, 1), 1) < STRIP

            def joined(mine, theirs, here):
                return jnp.where(strip_rows & (lanes < 64) & (here > 0), mine + theirs, mine)

            lanes = iota((1, 1, LANES), 2)
            half = members // 2

            def unpacked(r, d):
                at = d * (half + first)
                block = r[at : at + half]
                return jnp.concatenate([block, pltpu.roll(block, 64, 2)], axis=0)

            for d in range(levels):
                at = slice(d * members, (d + 1) * members)
                q = q_in[d]
                out[at, 0:16, :] = joined(q[:, 0:16, :], unpacked(recv[0], d), has_lo)
                for r0 in range(16, cx, 16):
                    out[at, r0 : r0 + 16, :] = q[:, r0 : r0 + 16, :]
                out[at, cx : cx + 16, :] = joined(q[:, cx : cx + 16, :], unpacked(recv[-1], d), has_hi)
            if first:
                rows16 = iota((16, LANES), 0) < STRIP
                more = lanes[0] >= 64
                ok_lo, ok_hi = rows16 & more & (has_lo > 0), rows16 & more & (has_hi > 0)
                out[0, 0:16] = out[0, 0:16] + jnp.where(ok_lo, recv[0][half], 0.0)
                out[0, cx : cx + 16] = out[0, cx : cx + 16] + jnp.where(ok_hi, recv[-1][half], 0.0)
            nxt = jnp.zeros((groups, exp, LANES), F32)
            prv = jnp.zeros((groups, exp, LANES), F32)

            def within(start, wide):
                return ((lanes - start) & (LANES - 1)) < wide

            for p in range(packs):
                block = out[p * groups : (p + 1) * groups]
                at = p * width
                wide = HALO if last else STRIP
                moved = pltpu.roll(block, at, 2) if at else block
                prv = jnp.where(within(at, wide), moved, prv)
                nxt = jnp.where(within(at + src_hi, wide), moved, nxt)
                if not last:
                    low = block - block.astype(BF16).astype(F32)
                    here = within(at + STRIP, HALO)
                    prv = jnp.where(here, pltpu.roll(low, (at + STRIP - HALO) % LANES, 2), prv)
                    here = within(at + src_hi + STRIP, HALO)
                    nxt = jnp.where(here, pltpu.roll(low, (at + STRIP) % LANES, 2), nxt)
            if not first:
                tail = rows_of((exp, LANES), ex, [*thirds(total[0:1]), *thirds(total[1:2])])[None]
                row = iota((1, exp, 1), 1) >= ex
                nxt = jnp.where(row, tail, nxt)
                prv = jnp.where(row, tail, prv)
            to_even[0:groups] = jnp.where(flip, prv, nxt).astype(kind)
            to_odd[0:groups] = jnp.where(flip, nxt, prv).astype(kind)
            if first:
                prv = pltpu.roll(out[0], LANES - 64, 1)
                nxt = pltpu.roll(out[0], LANES - 64 - cy, 1)
                to_even[groups] = jnp.where(flip, prv, nxt).astype(kind)
                to_odd[groups] = jnp.where(flip, nxt, prv).astype(kind)

        shapes = [sds(full_q, F32)] + [sds((groups + first, exp, LANES), kind)] * 2 + ([] if first else [small])
        ins = (1 if first else levels + 1) + n_strips
        return call(body, ins, shapes)

    far = list(range(2, n_lat - 1))

    def gathered(ix, q, from_prev, from_next, p, last):
        width = HALO if last else PACK
        groups, _ = packing(width)
        has_lo, has_hi = masks(ix, 2, n_lat)
        lane = iota((1, 1, LANES), 2)
        mine = q[p * groups : (p + 1) * groups]
        from_prev, from_next = from_prev[0:groups], from_next[0:groups]

        def put(total, packed, start, here, wide, where):
            ok = (lane >= start) & (lane < start + wide) & (here > 0)
            return total + jnp.where(ok, pltpu.roll(packed, (start - where) % LANES, 2), 0.0)

        at = p * width
        if last:
            mine = put(mine, from_prev, HALO, has_lo, HALO, at + cy + HALO)
            return put(mine, from_next, cy, has_hi, HALO, at)
        mine = put(mine, from_prev, 0, has_lo, STRIP, at + cy)
        return put(mine, from_next, cy, has_hi, STRIP, at)

    def with_low(from_prev, from_next):
        lane = iota((1, 1, LANES), 2)
        own_prev = ((lane - cy) & (LANES - 1)) % PACK < HALO
        place = lane % PACK
        own_next = (place >= HALO) & (place < STRIP)
        low_prev = pltpu.roll(from_prev, LANES - STRIP, 2)
        low_next = pltpu.roll(from_next, LANES - HALO, 2)
        return from_prev + jnp.where(own_prev, low_prev, 0.0), from_next + jnp.where(own_next, low_next, 0.0)

    def own_cells():
        row, lane = iota((exp, LANES), 0), iota((exp, LANES), 1)
        inside = (row >= HALO) & (row < HALO + cx) & (lane >= HALO) & (lane < HALO + cy)
        return inside.astype(F32)

    def sorted_by_side(ix, even, odd):
        flip = lax.rem(ix[2], 2) == 1
        e, o = even[...].astype(F32), odd[...].astype(F32)
        return jnp.where(flip, e, o), jnp.where(flip, o, e)

    def start_body(ix, q, even, odd, g_out, keep_out, gg):
        groups, packs = packing(PACK)
        from_prev, from_next = sorted_by_side(ix, even, odd)
        has_lo, has_hi = masks(ix, 2, n_lat)
        lane = iota((exp, LANES), 1)
        row = iota((exp, LANES), 0)
        mine = pltpu.roll(q[0], LANES - 64, 1)
        lo = from_prev[groups]
        hi = pltpu.roll(from_next[groups], cy, 1)
        keep = jnp.where(lane < ey, mine, 0.0)
        keep = keep + jnp.where((lane < STRIP) & (has_lo > 0), lo, 0.0)
        keep = keep + jnp.where((lane >= cy) & (lane < ey) & (has_hi > 0), hi, 0.0)
        keep = jnp.where(row < ex, keep, 0.0)
        from_prev, from_next = with_low(from_prev, from_next)
        keep_out[...] = keep
        acc = jnp.zeros((exp, LANES), F32)
        for p in range(packs):
            g = -(keep[None] * gathered(ix, q, from_prev, from_next, p, False))
            g_out[p * groups : (p + 1) * groups] = g
            acc = acc + jnp.sum(g * g, axis=0)
        gg[...] = jnp.broadcast_to(jnp.sum(acc * own_cells()), (8, LANES))

    g_shape = sds(full_q, F32)
    start_step = call(start_body, 3, [g_shape, sds((exp, LANES), F32), small])
    final_shape = sds((members, levels, cx, cy), F32)

    def step(first, last):
        groups, packs = packing(HALO if last else PACK)

        def body(ix, q, even, odd, sums, keep, g, *rest):
            tiny, rest = rest[: len(far)], rest[len(far) :]
            if not first:
                c_in, rest = rest[0], rest[1:]
            g_out, c_out = rest[:2]
            from_prev, from_next = sorted_by_side(ix, even, odd)
            if not last:
                from_prev, from_next = with_low(from_prev, from_next)
            total = sums[...]
            for ref in tiny:
                total = total + ref[...]
            gg, dot = total[0:1], total[1:2]
            for ref in [even, odd] if n_lat > 2 else [even]:
                more = tail_sums(ref[0], ex)
                gg, dot = gg + more[0], dot + more[1]
            alpha = (gg / (gg + dot))[None]
            kept = keep[...][None]
            acc = jnp.zeros((exp, LANES), F32)
            for p in range(packs):
                at = slice(p * groups, (p + 1) * groups)
                old = g[at]
                image = old + kept * gathered(ix, q, from_prev, from_next, p, last)
                new = old - alpha * image
                ctl = -alpha * old if first else c_in[at] - alpha * old
                if not last:
                    g_out[at] = new
                    c_out[at] = ctl
                    acc = acc + jnp.sum(new * new, axis=0)
                else:
                    for ref, val in ((g_out, new), (c_out, ctl)):
                        val = pltpu.roll(val[:, HALO : HALO + cx], LANES - HALO, 2)
                        for i in range(groups):
                            f = p * groups + i
                            ref[f % members, level(f // members, ix)] = val[i, :, :cy]
            if not last:
                rest[2][...] = jnp.broadcast_to(jnp.sum(acc * own_cells()), (8, LANES))

        shapes = [final_shape] * 2 if last else [g_shape, g_shape, small]
        return call(body, 6 + len(far) + (not first), shapes)

    def ring(size, d):
        return [(i, (i + d) % size) for i in range(size)]

    def partner(d):
        return [(i, i ^ d) for i in range(n_mem)]

    even_pairs = [(i, i ^ 1) for i in range(n_lat)]
    odd_pairs = [((i + 1) % n_lat, ((i ^ 1) + 1) % n_lat) for i in range(n_lat)]

    def exchange(qs, strips, sc, first, last):
        if n_lon == 2:
            recv = [lax.ppermute(strips[0], "lon", ring(2, 1))]
        else:
            recv = [lax.ppermute(strips[0], "lon", ring(n_lon, 1)), lax.ppermute(strips[1], "lon", ring(n_lon, -1))]
        out, to_even, to_odd, *sums = lon_join(first, last)(*qs, *sc, *recv)
        if not first and n_lon > 2:
            for d in range(2, n_lon - 1):
                sums[0] = sums[0] + lax.ppermute(sc[0], "lon", ring(n_lon, d))
        tiny = [] if first else [lax.ppermute(sums[0], "lat", ring(n_lat, d)) for d in far]
        even = lax.ppermute(to_even, "lat", even_pairs)
        odd = lax.ppermute(to_odd, "lat", odd_pairs)
        return out, even, odd, sums, tiny

    def local(ensemble, huber, innovation, sea_mask):
        slot = lax.broadcasted_iota(jnp.int32, (3,), 0)
        ix = jnp.where(
            slot == 0,
            lax.axis_index("mem"),
            jnp.where(slot == 1, lax.axis_index("lon"), lax.axis_index("lat")),
        ).astype(jnp.int32)
        far_off = [pltpu.with_memory_space_constraint(x, pltpu.HBM) for x in (ensemble, huber, innovation, at_tab, bn_tab, sea_mask)]
        q, recip, *strips = first_adjoint(ix, *far_off)
        q, r_prev, r_next, _, _ = exchange([q], strips, [], True, False)
        g, keep, gg = start_step(q, r_prev, r_next)
        control = []
        sends = list(range(n_mem - 1, 0, -1))
        for it in range(ITERS):
            last = it == ITERS - 1
            parts = {d: forward(d)(ensemble, g, keep, a_tab, bt_tab, gg)[0] for d in sends + [0]}
            moved = {d: lax.ppermute(parts[d], "mem", partner(d)) for d in sends}
            mis, ggm = misfit_own(huber, parts[0], *[moved[d] for d in sends])
            every = {d: lax.ppermute(mis, "mem", partner(d)) for d in sends}
            every[0] = mis
            qs, dots = [], []
            for d in order[:-1]:
                q, dot = adjoint(d, 0)(ensemble, recip, at_tab, bn_tab, every[d])
                qs.append(q)
                dots.append(dot)
            d = order[-1]
            q, sc, *strips = adjoint(d, levels - 1)(
                ensemble, recip, at_tab, bn_tab, every[d], ggm, *qs, *dots
            )
            by_level = dict(zip(order, qs + [q]))
            q, r_prev, r_next, sums, tiny = exchange([by_level[d] for d in range(levels)], strips, [sc], False, last)
            out = step(it == 0, last)(q, r_prev, r_next, *sums, keep, g, *tiny, *control)
            if last:
                return out[1], out[0]
            g, control, gg = out[0], [out[1]], out[2]

    return local


def solution(mesh):
    placed = (
        P("mem", None, None, "lon", "lat"),
        P(None, None, "lon", "lat"),
        P(None, None, "lon", "lat"),
        P("lon", "lat"),
    )

    def local(ensemble, huber, innovation, sea_mask):
        return build(dict(mesh.shape), ensemble.shape, sea_mask.shape)(ensemble, huber, innovation, sea_mask)

    return jax.shard_map(
        local,
        mesh=mesh,
        in_specs=placed,
        out_specs=(P("mem", None, "lon", "lat"), P("mem", None, "lon", "lat")),
        check_vma=False,
    )
```
